256 devices in a mesh: dp: 4 (over y), tensor: 16 (over x, z_hi, core), section: 4 (over z_lo).
Axes of the slice: x: 4, y: 4, z: 8 (z_hi: 2, z_lo: 4; z = z_hi * 4 + z_lo), core: 2. Of those that a mesh axis runs over, the one named last changes fastest.
Arguments:
- sent_grads: bfloat16 [4, 4, 2, 384, 8192], P('section', 'dp', None, 'tensor'), may hold values from -0.15917969 to 0.15917969
- attn_out: bfloat16 [4, 4, 2, 384, 8192], P('section', 'dp', None, None, 'tensor'), may hold values from -6 to 6
- b_order: int32 [4, 2], replicated, may hold values from 0 to 1, each once within a row
Outputs:
- grad_wo: bfloat16 [4, 8192, 8192], P('section', 'dp', 'tensor')
The draws below stay inside these ranges and needn't reach their ends.
Inputs may be any that keep to these rules, and one draw needn't show every extreme that they name: Each row of b_order is a permutation of the 2 micro-batches.
All inputs are finite; a program needn't handle non-finite values.
Results may differ from the reference program's by a relative error of at most 0.013.
Values may be sent and summed in bfloat16 or wider, within the bound.
A program may use at most 128 MiB of HBM per device.

```python
import jax
import jax.numpy as jnp
from jax import lax

D = 8192
TOK = 384
MB = 2
QW = 8192
N_DP = 4
N_SECTION = 4


def strengthened(result, stream_key, source, target, blocks, factor):
    owner, partner = [(jnp.arange(result.shape[position]) // (result.shape[position] // blocks)).reshape([-1 if axis == position else 1 for axis in range(result.ndim)]) for position in (source, target)]
    chosen = jax.random.permutation(stream_key, blocks)[partner]
    strong = (owner == chosen) | (owner == (partner + blocks // 2) % blocks)
    return jnp.where(strong, factor * result, result)


def level_of(own_key, shape, pieces, low, top_value):
    loudness, own = 1.0, jax.random.fold_in(own_key, 6)
    for dim, shards_of in pieces:
        draws = jnp.exp(jax.random.uniform(jax.random.fold_in(own, dim), (shards_of,), jnp.float32, low / len(pieces), top_value / len(pieces)))
        loudness = loudness * jnp.repeat(draws, shape[dim] // shards_of).reshape([-1 if axis == dim else 1 for axis in range(len(shape))])
    return loudness


def noise(rng, extent, deviation, reach, cuts=(), kind=jnp.bfloat16):
    result = jax.random.normal(rng, extent, jnp.float32) * deviation
    if len(cuts) > 0:
        result = level_of(rng, extent, cuts, -0.22, 0.18) * result
    return jnp.clip(result, min=-reach, max=reach).astype(kind)


def noise_with(rng, dims, spread, bound, cuts, heavy, kind=jnp.bfloat16):
    result = spread * jax.random.normal(rng, dims, jnp.float32)
    if cuts:
        result = result * level_of(rng, dims, cuts, -0.22, 0.18)
    return jnp.clip(strengthened(result, jax.random.fold_in(rng, 3), *heavy), -bound, bound).astype(kind)


def setup_inputs(seed: int = 0) -> dict:
    arg_keys = jax.random.split(jax.random.key(seed), 4)
    sent_grads = noise_with(arg_keys[0], (N_SECTION, N_DP, MB, TOK, D), 0.02, 0.15917969, ((0, 4), (1, 4), (3, 16)), (1, 4, 4, 2.0))
    attn_out = noise(arg_keys[1], (N_SECTION, N_DP, MB, TOK, QW), 1.0, 6.0, ((0, 4), (1, 4), (4, 16)))
    b_order = jax.vmap(lambda own: jax.random.permutation(own, MB))(jax.random.split(arg_keys[2], N_SECTION)).reshape((N_SECTION, MB)).astype(jnp.int32)
    return dict(sent_grads=sent_grads, attn_out=attn_out, b_order=b_order)


def contract(left_side, right_side):
    return lax.dot_general(left_side, right_side, (((0,), (0,)), ((), ())), preferred_element_type=jnp.float32)


def reference(sent_grads, attn_out, b_order):
    micro_ids = jnp.arange(MB, dtype=jnp.int32)
    all_out = []
    for section_id in range(N_SECTION):
        upper_section = (section_id + 1) % N_SECTION
        matches = b_order[upper_section][None, :] == micro_ids[:, None]
        total_out = jnp.zeros((D, QW), jnp.float32)
        for replica in range(N_DP):
            received = sent_grads[upper_section, replica]
            zero_value = jnp.zeros((), received.dtype)
            out_grads = jnp.sum(jnp.where(matches[:, :, None, None], received[None], zero_value), axis=1).astype(received.dtype)
            flat_grads = out_grads.reshape(MB * TOK, D)
            flat_heads = attn_out[section_id, replica].reshape(MB * TOK, QW)
            out_part = lax.optimization_barrier(contract(flat_grads, flat_heads).astype(jnp.bfloat16))
            total_out = total_out + out_part.astype(jnp.float32)
        all_out.append(total_out.astype(jnp.bfloat16))
    return jnp.stack(all_out)
```

```python
import jax
import jax.numpy as jnp
from jax import lax
from jax.experimental import pallas as pl
from jax.experimental.pallas import tpu as pltpu
from jax.sharding import PartitionSpec as P

MESH = pl.DeviceIdType.MESH
N_DP, N_TENSOR, N_SECTION = 4, 16, 4
PIECE = 48
ROWS = N_TENSOR * PIECE
COLS = 2048
HALF = COLS // 2
WIDTH = 512
TILE = 256


def wrap(value, size):
    return lax.rem(value + size, size)


def kernel(
    grads, heads, out, a_all, b_all, acc,
    own_b, s1s, s1r, x1s, x1r, x2s, x2r, dds, ddr, b1s, b1r, b2s, b2r,
):
    y = lax.axis_index("dp")
    t = lax.axis_index("tensor")
    s = lax.axis_index("section")
    x = lax.div(t, 4)
    h = lax.rem(lax.div(t, 2), 2)
    c = lax.rem(t, 2)
    down, up = wrap(s - 1, 4), wrap(s + 1, 4)
    to_h = [wrap(h + lax.div(3 - s, 3) + n, 2) for n in (0, 1)]
    from_h = [wrap(h + lax.div(s, 3) + n, 2) for n in (0, 1)]

    def tensor_of(xx, hh, cc):
        return xx * 4 + hh * 2 + cc

    def rows_of(replica, source):
        return pl.ds(pl.multiple_of((replica * N_TENSOR + source) * PIECE, 16), PIECE)

    x_right, x_left, x_far = wrap(x + 1, 4), wrap(x - 1, 4), wrap(x + 2, 4)
    right, left = tensor_of(x_right, h, c), tensor_of(x_left, h, c)
    sibling = tensor_of(x, h, 1 - c)
    y_up, y_down, y_far = wrap(y + 1, 4), wrap(y - 1, 4), wrap(y + 2, 4)

    barrier = pltpu.get_barrier_semaphore()

    def greet(device):
        pl.semaphore_signal(barrier, inc=1, device_id=device, device_id_type=MESH)

    for j in range(4):
        for n in (0, 1):
            greet({"dp": wrap(y - j, 4), "tensor": tensor_of(x, from_h[n], c), "section": up})
    for device in (right, left, sibling):
        greet({"tensor": device})
    for device in (y_up, y_down):
        greet({"dp": device})
    pl.semaphore_wait(barrier, 13)

    def remote(src, dst, send, recv, device):
        return pltpu.make_async_remote_copy(
            src_ref=src, dst_ref=dst, send_sem=send, recv_sem=recv,
            device_id=device, device_id_type=MESH,
        )

    sends = []

    def go(copy):
        copy.start()
        sends.append(copy)

    def stage1(p):
        j, n = p // 2, p % 2
        target = wrap(y + j, 4)
        return remote(
            grads.at[:, pl.ds(pl.multiple_of(target * COLS, COLS), COLS)],
            a_all.at[rows_of(y, t), :],
            s1s.at[p], s1r.at[p],
            {"dp": target, "tensor": tensor_of(x, to_h[n], c), "section": down},
        )

    def stored(p, xx, cc, half=None):
        j, n = p // 2, p % 2
        rows = rows_of(wrap(y - j, 4), tensor_of(xx, from_h[n], cc))
        return a_all.at[rows, :] if half is None else a_all.at[rows, pl.ds(half * HALF, HALF)]

    def hop1(p, way, xx):
        block = stored(p, xx, c)
        return remote(block, block, x1s.at[p, way], x1r.at[p, way], {"tensor": (right, left)[way]})

    def hop2(p, way, xx):
        block = stored(p, xx, c, way)
        return remote(block, block, x2s.at[p, way], x2r.at[p, way], {"tensor": (right, left)[way]})

    def across(p, kind, cc):
        xx = (x, x_left, x_right, x_far)[kind]
        block = stored(p, xx, cc)
        return remote(block, block, dds.at[p, kind], ddr.at[p, kind], {"tensor": sibling})

    def b_rows(replica, half=None):
        if half is None:
            return b_all.at[pl.ds(pl.multiple_of(replica * ROWS, ROWS), ROWS), :]
        return b_all.at[pl.ds(pl.multiple_of(replica * ROWS + half * (ROWS // 2), 128), ROWS // 2), :]

    def b_hop1(way, src, replica):
        return remote(src, b_rows(replica), b1s.at[way], b1r.at[way], {"dp": (y_up, y_down)[way]})

    def b_hop2(way, replica):
        block = b_rows(replica, way)
        return remote(block, block, b2s.at[way], b2r.at[way], {"dp": (y_up, y_down)[way]})

    def compute(j):
        replica = wrap(y - j, 4)
        rows = pl.ds(pl.multiple_of(replica * ROWS, ROWS), ROWS)

        def tile(m, carry):
            columns = pl.ds(pl.multiple_of(m * TILE, TILE), TILE)
            part = lax.dot_general(
                a_all[rows, columns], b_all[rows, :], (((0,), (0,)), ((), ())),
                preferred_element_type=jnp.float32,
            )
            if j == 0:
                acc[columns, :] = part
            elif j < 3:
                acc[columns, :] += part
            else:
                out[columns, :] = (acc[columns, :] + part).astype(out.dtype)
            return carry

        lax.fori_loop(0, COLS // TILE, tile, 0)

    for p in range(8):
        go(stage1(p))
    own = pltpu.make_async_copy(heads, b_rows(y), own_b)
    own.start()
    for way in (0, 1):
        go(b_hop1(way, heads, y))

    def first(p):
        stage1(p).wait_recv()
        go(hop1(p, 0, x))
        go(hop1(p, 1, x))
        go(across(p, 0, c))

    def second(p):
        hop1(p, 0, x_left).wait_recv()
        go(hop2(p, 0, x_left))
        go(across(p, 1, c))
        hop1(p, 1, x_right).wait_recv()
        go(hop2(p, 1, x_right))
        go(across(p, 2, c))

    def third(p):
        hop2(p, 0, x_far).wait_recv()
        hop2(p, 1, x_far).wait_recv()
        go(across(p, 3, c))

    def finish(j):
        for p in (2 * j, 2 * j + 1):
            for kind in range(4):
                across(p, kind, 1 - c).wait_recv()
        if j == 2:
            for way in (0, 1):
                b_hop2(way, y_far).wait_recv()
        compute(j)

    for step in range(11):
        if step < 8:
            first(step)
        if 1 <= step < 9:
            second(step - 1)
        if 2 <= step < 10:
            third(step - 2)
        if step == 3:
            own.wait()
            b_hop1(0, heads, y_down).wait_recv()
            go(b_hop2(0, y_down))
            b_hop1(1, heads, y_up).wait_recv()
            go(b_hop2(1, y_up))
        if step >= 4 and step % 2 == 0:
            finish((step - 4) // 2)
    for copy in sends:
        copy.wait_send()


def on_device(sent_grads, attn_out, b_order):
    s = lax.axis_index("section")
    order = lax.dynamic_index_in_dim(b_order, lax.rem(s + 1, N_SECTION), 0, keepdims=False)
    grads = sent_grads[0, 0].reshape(PIECE, N_DP * COLS)
    heads = attn_out[0, 0]
    in_slots = jnp.stack([jnp.where(order[k] == 0, heads[0], heads[1]) for k in range(2)])
    in_slots = in_slots.reshape(2, N_TENSOR, PIECE // 2, WIDTH).transpose(1, 0, 2, 3).reshape(ROWS, WIDTH)
    dma = pltpu.SemaphoreType.DMA
    result = pl.pallas_call(
        kernel,
        out_shape=jax.ShapeDtypeStruct((COLS, WIDTH), jnp.bfloat16),
        in_specs=[pl.BlockSpec(memory_space=pl.ANY)] * 2,
        out_specs=pl.BlockSpec(memory_space=pltpu.VMEM),
        scratch_shapes=[
            pltpu.VMEM((N_DP * ROWS, COLS), jnp.bfloat16),
            pltpu.VMEM((N_DP * ROWS, WIDTH), jnp.bfloat16),
            pltpu.VMEM((COLS, WIDTH), jnp.float32),
            dma, dma((8,)), dma((8,)), dma((8, 2)), dma((8, 2)), dma((8, 2)), dma((8, 2)),
            dma((8, 4)), dma((8, 4)), dma((2,)), dma((2,)), dma((2,)), dma((2,)),
        ],
        compiler_params=pltpu.CompilerParams(
            collective_id=0, has_side_effects=True, vmem_limit_bytes=48 * 2**20
        ),
    )(grads, in_slots)
    return result[None]


def solution(mesh):
    placed = (
        P("section", "dp", None, "tensor", None),
        P("section", "dp", None, None, "tensor"),
        P(),
    )
    return jax.shard_map(
        on_device,
        mesh=mesh,
        in_specs=placed,
        out_specs=P("section", "dp", "tensor"),
        check_vma=False,
    )
```

```python
import jax
import jax.numpy as jnp
from jax import lax
from jax.experimental import pallas as pl
from jax.experimental.pallas import tpu as pltpu
from jax.sharding import PartitionSpec as P

MESH = pl.DeviceIdType.MESH
N_DP, N_TENSOR, N_SECTION = 4, 16, 4
TOKENS = 24
PIECE = 2 * TOKENS
GROUP = 8 * PIECE
ROWS = N_TENSOR * PIECE
COLS = 2048
HALF = COLS // 2
WIDTH = 512
TILE = 2048
NEAR, FAR = 0, 1
RELAYED = (0, FAR)
ORDER = ((0, NEAR), (3, NEAR), (1, NEAR), (3, FAR), (2, NEAR), (1, FAR), (2, FAR), (0, FAR))
PARTS = 2


PLAN = (
    ("send", (0, NEAR)),
    ("send", (3, FAR)),
    ("send", (3, NEAR)),
    ("send", (1, FAR)),
    ("send", (1, NEAR)),
    ("send", (2, FAR)),
    ("send", (2, NEAR)),
    ("first", (0, NEAR)),
    ("first", (3, NEAR)),
    ("heads", None),
    ("first", (1, NEAR)),
    ("second", (0, NEAR)),
    ("first", (3, FAR)),
    ("second", (3, NEAR)),
    ("third", (0, NEAR)),
    ("first", (2, NEAR)),
    ("second", (1, NEAR)),
    ("third", (3, NEAR)),
    ("finish", (0, NEAR)),
    ("relay", None),
    ("first", (1, FAR)),
    ("second", (3, FAR)),
    ("third", (1, NEAR)),
    ("first", (2, FAR)),
    ("second", (2, NEAR)),
    ("third", (3, FAR)),
    ("heads2", None),
    ("finish", (3, NEAR)),
    ("first", (0, FAR)),
    ("second", (1, FAR)),
    ("third", (2, NEAR)),
    ("finish", (1, NEAR)),
    ("finish", (3, FAR)),
    ("second", (2, FAR)),
    ("third", (1, FAR)),
    ("second", (0, FAR)),
    ("third", (2, FAR)),
    ("heads3", None),
    ("finish", (2, NEAR)),
    ("finish", (1, FAR)),
    ("third", (0, FAR)),
    ("finish", (2, FAR)),
    ("finish", (0, FAR)),
)


def wrap(value, size):
    return lax.rem(value + size, size)


def kernel(
    order, grads, heads, out, a_all, b_all, acc, staged, heads_in, done,
    own_h, qs, qr, q1s, q1r, outs, s1s, s1r, rs, rr, x1s, x1r, x2s, x2r, dds, ddr, b1s, b1r, b2s, b2r,
):
    y = lax.axis_index("dp")
    t = lax.axis_index("tensor")
    s = lax.axis_index("section")
    x = lax.div(t, 4)
    h = lax.rem(lax.div(t, 2), 2)
    c = lax.rem(t, 2)
    z = 4 * h + s
    down, up = wrap(s - 1, 4), wrap(s + 1, 4)

    def tensor_of(xx, hh, cc):
        return xx * 4 + hh * 2 + cc

    def at_z(zz):
        return {"tensor": tensor_of(x, lax.div(zz, 4), c), "section": lax.rem(zz, 4)}

    to_z = (wrap(z - 1, 8), wrap(z + 3, 8))
    from_z = (wrap(z + 1, 8), wrap(z - 3, 8))
    from_h = tuple(lax.div(zz, 4) for zz in from_z)

    def rows_of(replica, xx, hh, cc):
        slot = replica * N_TENSOR + hh * 8 + xx * 2 + cc
        return pl.ds(pl.multiple_of(slot * PIECE, 16), PIECE)

    x_right, x_left, x_far = wrap(x + 1, 4), wrap(x - 1, 4), wrap(x + 2, 4)
    x_to = ({"tensor": tensor_of(x_right, h, c)}, {"tensor": tensor_of(x_left, h, c)})
    sibling = {"tensor": tensor_of(x, h, 1 - c)}
    y_up, y_down, y_far = wrap(y + 1, 4), wrap(y - 1, 4), wrap(y + 2, 4)
    y_to = ({"dp": y_up}, {"dp": y_down})

    own = pltpu.make_async_copy(heads, heads_in, own_h)
    own.start()

    barrier = pltpu.get_barrier_semaphore()

    def greet(device):
        pl.semaphore_signal(barrier, inc=1, device_id=device, device_id_type=MESH)

    for j in range(4):
        for n in (NEAR, FAR):
            if (j, n) != RELAYED:
                greet({"dp": wrap(y - j, 4), **at_z(from_z[n])})
    greet(at_z(wrap(z + 2, 8)))
    for device in (*x_to, sibling, *y_to):
        greet(device)
    pl.semaphore_wait(barrier, 13)

    def remote(src, dst, send, recv, device):
        return pltpu.make_async_remote_copy(
            src_ref=src, dst_ref=dst, send_sem=send, recv_sem=recv,
            device_id=device, device_id_type=MESH,
        )

    sends = []

    def go(copy):
        copy.start()
        sends.append(copy)

    def index(piece):
        return piece[0] * 2 + piece[1]

    def stage1(piece, part=None):
        j, n = piece
        target = wrap(y + j, 4)
        size = COLS if part is None else COLS // PARTS
        start = 0 if part is None else part * size
        return remote(
            grads.at[:, pl.ds(pl.multiple_of(target * COLS + start, size), size)],
            a_all.at[rows_of(y, x, h, c), pl.ds(start, size)],
            s1s.at[index(piece)] if part is None else qs.at[part],
            s1r.at[index(piece)] if part is None else qr.at[part],
            {"dp": target, **at_z(to_z[n])},
        )

    def stored(piece, xx, cc, half=None):
        j, n = piece
        rows = rows_of(wrap(y - j, 4), xx, from_h[n], cc)
        return a_all.at[rows, :] if half is None else a_all.at[rows, pl.ds(half * HALF, HALF)]

    def relay1():
        return remote(stored((RELAYED[0], NEAR), x, c), staged, rs.at[0], rr.at[0], at_z(wrap(z - 2, 8)))

    def relay2():
        rows = rows_of(wrap(y - RELAYED[0], 4), x, lax.div(wrap(z + 3, 8), 4), c)
        return remote(staged, a_all.at[rows, :], rs.at[1], rr.at[1], at_z(wrap(z - 2, 8)))

    def hop1(piece, way, xx, part=None):
        block = stored(piece, xx, c)
        if part is None:
            return remote(block, block, x1s.at[index(piece), way], x1r.at[index(piece), way], x_to[way])
        block = block.at[:, pl.ds(part * (COLS // PARTS), COLS // PARTS)]
        return remote(block, block, q1s.at[part, way], q1r.at[part, way], x_to[way])

    def hop2(piece, way, xx):
        block = stored(piece, xx, c, way)
        return remote(block, block, x2s.at[index(piece), way], x2r.at[index(piece), way], x_to[way])

    def across(piece, kind, cc):
        block = stored(piece, (x, x_left, x_right, x_far)[kind], cc)
        return remote(block, block, dds.at[index(piece), kind], ddr.at[index(piece), kind], sibling)

    def b_rows(replica, half=0, size=ROWS):
        return b_all.at[pl.ds(pl.multiple_of(replica * ROWS + half * (ROWS // 2), 128), size), :]

    def b_hop1(way, replica):
        block = b_rows(replica)
        return remote(block, block, b1s.at[way], b1r.at[way], y_to[way])

    def b_hop2(way, replica):
        block = b_rows(replica, way, ROWS // 2)
        return remote(block, block, b2s.at[way], b2r.at[way], y_to[way])

    def order_heads():
        own.wait()
        slots = (order[0, up], order[1, up])

        def place(slot, carry):
            source = tensor_of(lax.rem(lax.div(slot, 2), 4), lax.div(slot, 8), lax.rem(slot, 2))
            parts = [heads_in[m, source].astype(jnp.float32) for m in slots]
            rows = pl.ds(pl.multiple_of(y * ROWS + slot * PIECE, 16), PIECE)
            b_all[rows, :] = jnp.concatenate(parts, axis=0).astype(b_all.dtype)
            return carry

        lax.fori_loop(0, N_TENSOR, place, 0)

    def write(m):
        columns = pl.ds(pl.multiple_of(m * TILE, TILE), TILE)
        return pltpu.make_async_copy(done.at[columns, :], out.at[columns, :], outs.at[m])

    def compute(piece, first, last):
        j, n = piece
        start = wrap(y - j, 4) * ROWS + from_h[n] * GROUP
        rows = pl.ds(pl.multiple_of(start, GROUP), GROUP)

        def tile(m, carry):
            columns = pl.ds(pl.multiple_of(m * TILE, TILE), TILE)
            part = lax.dot_general(
                a_all[rows, columns], b_all[rows, :], (((0,), (0,)), ((), ())),
                preferred_element_type=jnp.float32,
            )
            if first:
                acc[columns, :] = part
            elif last:
                done[columns, :] = (acc[columns, :] + part).astype(done.dtype)
                write(m).start()
            else:
                acc[columns, :] += part
            return carry

        lax.fori_loop(0, COLS // TILE, tile, 0)

    def first(piece):
        if piece == ORDER[0]:
            for part in range(PARTS):
                stage1(piece, part).wait_recv()
                go(hop1(piece, 0, x, part))
                go(hop1(piece, 1, x, part))
            go(relay1())
        else:
            if piece == RELAYED:
                relay2().wait_recv()
            else:
                stage1(piece).wait_recv()
            go(hop1(piece, 0, x))
            go(hop1(piece, 1, x))
        go(across(piece, 0, c))

    def second(piece):
        for way, xx in ((0, x_left), (1, x_right)):
            if piece == ORDER[0]:
                for part in range(PARTS):
                    hop1(piece, way, xx, part).wait_recv()
            else:
                hop1(piece, way, xx).wait_recv()
            go(hop2(piece, way, xx))
            go(across(piece, 1 + way, c))

    def third(piece):
        hop2(piece, 0, x_far).wait_recv()
        hop2(piece, 1, x_far).wait_recv()
        go(across(piece, 3, c))

    def finish(piece):
        for kind in range(4):
            across(piece, kind, 1 - c).wait_recv()
        compute(piece, piece == ORDER[0], piece == ORDER[-1])

    paced = [piece for act, piece in PLAN if act == "sent"]
    for act, piece in PLAN:
        if act == "send":
            for copy in [stage1(piece, part) for part in range(PARTS)] if piece == ORDER[0] else [stage1(piece)]:
                copy.start()
                if piece not in paced:
                    sends.append(copy)
        elif act == "sent":
            stage1(piece).wait_send()
        elif act == "relay":
            relay1().wait_recv()
            go(relay2())
        elif act == "heads":
            order_heads()
            for way in (0, 1):
                go(b_hop1(way, y))
        elif act == "heads2":
            b_hop1(0, y_down).wait_recv()
            go(b_hop2(0, y_down))
            b_hop1(1, y_up).wait_recv()
            go(b_hop2(1, y_up))
        elif act == "heads3":
            for way in (0, 1):
                b_hop2(way, y_far).wait_recv()
        else:
            dict(first=first, second=second, third=third, finish=finish)[act](piece)
    for copy in sends:
        copy.wait_send()
    for m in range(COLS // TILE):
        write(m).wait()


def on_device(sent_grads, attn_out, b_order):
    grads = sent_grads[0, 0].reshape(PIECE, N_DP * COLS)
    heads = attn_out[0, 0].reshape(2, N_TENSOR, TOKENS, WIDTH)
    dma = pltpu.SemaphoreType.DMA
    result = pl.pallas_call(
        kernel,
        out_shape=jax.ShapeDtypeStruct((COLS, WIDTH), jnp.bfloat16),
        in_specs=[
            pl.BlockSpec(memory_space=pltpu.SMEM),
            pl.BlockSpec(memory_space=pltpu.HBM),
            pl.BlockSpec(memory_space=pltpu.HBM),
        ],
        out_specs=pl.BlockSpec(memory_space=pltpu.HBM),
        scratch_shapes=[
            pltpu.VMEM((N_DP * ROWS, COLS), jnp.bfloat16),
            pltpu.VMEM((N_DP * ROWS, WIDTH), jnp.bfloat16),
            pltpu.VMEM((COLS, WIDTH), jnp.float32),
            pltpu.VMEM((PIECE, COLS), jnp.bfloat16),
            pltpu.VMEM((2, N_TENSOR, TOKENS, WIDTH), jnp.bfloat16),
            pltpu.VMEM((COLS, WIDTH), jnp.bfloat16),
            dma, dma((PARTS,)), dma((PARTS,)), dma((PARTS, 2)), dma((PARTS, 2)), dma((COLS // TILE,)),
            dma((8,)), dma((8,)), dma((2,)), dma((2,)),
            dma((8, 2)), dma((8, 2)), dma((8, 2)), dma((8, 2)),
            dma((8, 4)), dma((8, 4)), dma((2,)), dma((2,)), dma((2,)), dma((2,)),
        ],
        compiler_params=pltpu.CompilerParams(
            collective_id=0, has_side_effects=True, vmem_limit_bytes=58 * 2**20
        ),
    )(b_order.T, grads, heads)
    return result[None]


def solution(mesh):
    placed = (
        P("section", "dp", None, "tensor", None),
        P("section", "dp", None, None, "tensor"),
        P(),
    )
    return jax.shard_map(
        on_device,
        mesh=mesh,
        in_specs=placed,
        out_specs=P("section", "dp", "tensor"),
        check_vma=False,
    )
```

```python
import jax
import jax.numpy as jnp
from jax import lax
from jax.experimental import pallas as pl
from jax.experimental.pallas import tpu as pltpu
from jax.sharding import PartitionSpec as P

MESH = pl.DeviceIdType.MESH
N_DP, N_TENSOR, N_SECTION = 4, 16, 4
TOKENS = 24
PIECE = 2 * TOKENS
GROUP = 8 * PIECE
ROWS = N_TENSOR * PIECE
COLS = 2048
HALF = COLS // 2
WIDTH = 512
TILE = 2048
NEAR, FAR = 0, 1
RELAYED = (0, FAR)
ORDER = ((0, NEAR), (3, NEAR), (1, NEAR), (3, FAR), (2, NEAR), (1, FAR), (2, FAR), (0, FAR))
PARTS = 2


PLAN = (
    ("send", (0, NEAR)),
    ("send", (3, FAR)),
    ("send", (3, NEAR)),
    ("send", (1, FAR)),
    ("send", (1, NEAR)),
    ("send", (2, FAR)),
    ("send", (2, NEAR)),
    ("first", (0, NEAR)),
    ("first", (3, NEAR)),
    ("heads", None),
    ("second", (0, NEAR)),
    ("first", (1, NEAR)),
    ("second", (3, NEAR)),
    ("first", (3, FAR)),
    ("third", (0, NEAR)),
    ("second", (1, NEAR)),
    ("first", (2, NEAR)),
    ("third", (3, NEAR)),
    ("finish", (0, NEAR)),
    ("second", (3, FAR)),
    ("first", (1, FAR)),
    ("third", (1, NEAR)),
    ("relay", None),
    ("second", (2, NEAR)),
    ("first", (2, FAR)),
    ("third", (3, FAR)),
    ("heads2", None),
    ("finish", (3, NEAR)),
    ("second", (1, FAR)),
    ("first", (0, FAR)),
    ("third", (2, NEAR)),
    ("finish", (1, NEAR)),
    ("finish", (3, FAR)),
    ("second", (2, FAR)),
    ("third", (1, FAR)),
    ("second", (0, FAR)),
    ("third", (2, FAR)),
    ("heads3", None),
    ("finish", (2, NEAR)),
    ("finish", (1, FAR)),
    ("third", (0, FAR)),
    ("finish", (2, FAR)),
    ("finish", (0, FAR)),
)


def wrap(value, size):
    return lax.rem(value + size, size)


def kernel(
    order, grads, heads, out, a_all, b_all, acc, staged, heads_in, done,
    own_h, qs, qr, q1s, q1r, outs, s1s, s1r, rs, rr, x1s, x1r, x2s, x2r, dds, ddr, b1s, b1r, b2s, b2r,
):
    y = lax.axis_index("dp")
    t = lax.axis_index("tensor")
    s = lax.axis_index("section")
    x = lax.div(t, 4)
    h = lax.rem(lax.div(t, 2), 2)
    c = lax.rem(t, 2)
    z = 4 * h + s
    down, up = wrap(s - 1, 4), wrap(s + 1, 4)

    def tensor_of(xx, hh, cc):
        return xx * 4 + hh * 2 + cc

    def at_z(zz):
        return {"tensor": tensor_of(x, lax.div(zz, 4), c), "section": lax.rem(zz, 4)}

    to_z = (wrap(z - 1, 8), wrap(z + 3, 8))
    from_z = (wrap(z + 1, 8), wrap(z - 3, 8))
    from_h = tuple(lax.div(zz, 4) for zz in from_z)

    def rows_of(replica, xx, hh, cc):
        slot = replica * N_TENSOR + hh * 8 + xx * 2 + cc
        return pl.ds(pl.multiple_of(slot * PIECE, 16), PIECE)

    x_right, x_left, x_far = wrap(x + 1, 4), wrap(x - 1, 4), wrap(x + 2, 4)
    x_to = ({"tensor": tensor_of(x_right, h, c)}, {"tensor": tensor_of(x_left, h, c)})
    sibling = {"tensor": tensor_of(x, h, 1 - c)}
    y_up, y_down, y_far = wrap(y + 1, 4), wrap(y - 1, 4), wrap(y + 2, 4)
    y_to = ({"dp": y_up}, {"dp": y_down})

    own = pltpu.make_async_copy(heads, heads_in, own_h)
    own.start()

    barrier = pltpu.get_barrier_semaphore()

    def greet(device):
        pl.semaphore_signal(barrier, inc=1, device_id=device, device_id_type=MESH)

    for j in range(4):
        for n in (NEAR, FAR):
            if (j, n) != RELAYED:
                greet({"dp": wrap(y - j, 4), **at_z(from_z[n])})
    greet(at_z(wrap(z + 2, 8)))
    for device in (*x_to, sibling, *y_to):
        greet(device)
    pl.semaphore_wait(barrier, 13)

    def remote(src, dst, send, recv, device):
        return pltpu.make_async_remote_copy(
            src_ref=src, dst_ref=dst, send_sem=send, recv_sem=recv,
            device_id=device, device_id_type=MESH,
        )

    sends = []

    def go(copy):
        copy.start()
        sends.append(copy)

    def index(piece):
        return piece[0] * 2 + piece[1]

    def stage1(piece, part=None):
        j, n = piece
        target = wrap(y + j, 4)
        size = COLS if part is None else COLS // PARTS
        start = 0 if part is None else part * size
        return remote(
            grads.at[:, pl.ds(pl.multiple_of(target * COLS + start, size), size)],
            a_all.at[rows_of(y, x, h, c), pl.ds(start, size)],
            s1s.at[index(piece)] if part is None else qs.at[part],
            s1r.at[index(piece)] if part is None else qr.at[part],
            {"dp": target, **at_z(to_z[n])},
        )

    def stored(piece, xx, cc, half=None):
        j, n = piece
        rows = rows_of(wrap(y - j, 4), xx, from_h[n], cc)
        return a_all.at[rows, :] if half is None else a_all.at[rows, pl.ds(half * HALF, HALF)]

    def relay1():
        return remote(stored((RELAYED[0], NEAR), x, c), staged, rs.at[0], rr.at[0], at_z(wrap(z - 2, 8)))

    def relay2():
        rows = rows_of(wrap(y - RELAYED[0], 4), x, lax.div(wrap(z + 3, 8), 4), c)
        return remote(staged, a_all.at[rows, :], rs.at[1], rr.at[1], at_z(wrap(z - 2, 8)))

    def hop1(piece, way, xx, part=None):
        block = stored(piece, xx, c)
        if part is None:
            return remote(block, block, x1s.at[index(piece), way], x1r.at[index(piece), way], x_to[way])
        block = block.at[:, pl.ds(part * (COLS // PARTS), COLS // PARTS)]
        return remote(block, block, q1s.at[part, way], q1r.at[part, way], x_to[way])

    def hop2(piece, way, xx):
        block = stored(piece, xx, c, way)
        return remote(block, block, x2s.at[index(piece), way], x2r.at[index(piece), way], x_to[way])

    def across(piece, kind, cc):
        block = stored(piece, (x, x_left, x_right, x_far)[kind], cc)
        return remote(block, block, dds.at[index(piece), kind], ddr.at[index(piece), kind], sibling)

    def b_rows(replica, half=0, size=ROWS):
        return b_all.at[pl.ds(pl.multiple_of(replica * ROWS + half * (ROWS // 2), 128), size), :]

    def b_hop1(way, replica):
        block = b_rows(replica)
        return remote(block, block, b1s.at[way], b1r.at[way], y_to[way])

    def b_hop2(way, replica):
        block = b_rows(replica, way, ROWS // 2)
        return remote(block, block, b2s.at[way], b2r.at[way], y_to[way])

    def order_heads():
        own.wait()
        slots = (order[0, up], order[1, up])

        def place(slot, carry):
            source = tensor_of(lax.rem(lax.div(slot, 2), 4), lax.div(slot, 8), lax.rem(slot, 2))
            parts = [heads_in[m, source].astype(jnp.float32) for m in slots]
            rows = pl.ds(pl.multiple_of(y * ROWS + slot * PIECE, 16), PIECE)
            b_all[rows, :] = jnp.concatenate(parts, axis=0).astype(b_all.dtype)
            return carry

        lax.fori_loop(0, N_TENSOR, place, 0)

    def write(m):
        columns = pl.ds(pl.multiple_of(m * TILE, TILE), TILE)
        return pltpu.make_async_copy(done.at[columns, :], out.at[columns, :], outs.at[m])

    def compute(piece, first, last):
        j, n = piece
        start = wrap(y - j, 4) * ROWS + from_h[n] * GROUP
        rows = pl.ds(pl.multiple_of(start, GROUP), GROUP)

        def tile(m, carry):
            columns = pl.ds(pl.multiple_of(m * TILE, TILE), TILE)
            part = lax.dot_general(
                a_all[rows, columns], b_all[rows, :], (((0,), (0,)), ((), ())),
                preferred_element_type=jnp.float32,
            )
            if first:
                acc[columns, :] = part
            elif last:
                done[columns, :] = (acc[columns, :] + part).astype(done.dtype)
                write(m).start()
            else:
                acc[columns, :] += part
            return carry

        lax.fori_loop(0, COLS // TILE, tile, 0)

    def first(piece):
        if piece == ORDER[0]:
            for part in range(PARTS):
                stage1(piece, part).wait_recv()
                go(hop1(piece, 0, x, part))
                go(hop1(piece, 1, x, part))
            go(relay1())
        else:
            if piece == RELAYED:
                relay2().wait_recv()
            else:
                stage1(piece).wait_recv()
            go(hop1(piece, 0, x))
            go(hop1(piece, 1, x))
        go(across(piece, 0, c))

    def second(piece):
        for way, xx in ((0, x_left), (1, x_right)):
            if piece == ORDER[0]:
                for part in range(PARTS):
                    hop1(piece, way, xx, part).wait_recv()
            else:
                hop1(piece, way, xx).wait_recv()
            go(hop2(piece, way, xx))
            go(across(piece, 1 + way, c))

    def third(piece):
        hop2(piece, 0, x_far).wait_recv()
        hop2(piece, 1, x_far).wait_recv()
        go(across(piece, 3, c))

    def finish(piece):
        for kind in range(4):
            across(piece, kind, 1 - c).wait_recv()
        compute(piece, piece == ORDER[0], piece == ORDER[-1])

    paced = [piece for act, piece in PLAN if act == "sent"]
    for act, piece in PLAN:
        if act == "send":
            for copy in [stage1(piece, part) for part in range(PARTS)] if piece == ORDER[0] else [stage1(piece)]:
                copy.start()
                if piece not in paced:
                    sends.append(copy)
        elif act == "sent":
            stage1(piece).wait_send()
        elif act == "relay":
            relay1().wait_recv()
            go(relay2())
        elif act == "heads":
            order_heads()
            for way in (0, 1):
                go(b_hop1(way, y))
        elif act == "heads2":
            b_hop1(0, y_down).wait_recv()
            go(b_hop2(0, y_down))
            b_hop1(1, y_up).wait_recv()
            go(b_hop2(1, y_up))
        elif act == "heads3":
            for way in (0, 1):
                b_hop2(way, y_far).wait_recv()
        else:
            dict(first=first, second=second, third=third, finish=finish)[act](piece)
    for copy in sends:
        copy.wait_send()
    for m in range(COLS // TILE):
        write(m).wait()


def on_device(sent_grads, attn_out, b_order):
    grads = sent_grads[0, 0].reshape(PIECE, N_DP * COLS)
    heads = attn_out[0, 0].reshape(2, N_TENSOR, TOKENS, WIDTH)
    dma = pltpu.SemaphoreType.DMA
    result = pl.pallas_call(
        kernel,
        out_shape=jax.ShapeDtypeStruct((COLS, WIDTH), jnp.bfloat16),
        in_specs=[
            pl.BlockSpec(memory_space=pltpu.SMEM),
            pl.BlockSpec(memory_space=pltpu.HBM),
            pl.BlockSpec(memory_space=pltpu.HBM),
        ],
        out_specs=pl.BlockSpec(memory_space=pltpu.HBM),
        scratch_shapes=[
            pltpu.VMEM((N_DP * ROWS, COLS), jnp.bfloat16),
            pltpu.VMEM((N_DP * ROWS, WIDTH), jnp.bfloat16),
            pltpu.VMEM((COLS, WIDTH), jnp.float32),
            pltpu.VMEM((PIECE, COLS), jnp.bfloat16),
            pltpu.VMEM((2, N_TENSOR, TOKENS, WIDTH), jnp.bfloat16),
            pltpu.VMEM((COLS, WIDTH), jnp.bfloat16),
            dma, dma((PARTS,)), dma((PARTS,)), dma((PARTS, 2)), dma((PARTS, 2)), dma((COLS // TILE,)),
            dma((8,)), dma((8,)), dma((2,)), dma((2,)),
            dma((8, 2)), dma((8, 2)), dma((8, 2)), dma((8, 2)),
            dma((8, 4)), dma((8, 4)), dma((2,)), dma((2,)), dma((2,)), dma((2,)),
        ],
        compiler_params=pltpu.CompilerParams(
            collective_id=0, has_side_effects=True, vmem_limit_bytes=58 * 2**20
        ),
    )(b_order.T, grads, heads)
    return result[None]


def solution(mesh):
    placed = (
        P("section", "dp", None, "tensor", None),
        P("section", "dp", None, None, "tensor"),
        P(),
    )
    return jax.shard_map(
        on_device,
        mesh=mesh,
        in_specs=placed,
        out_specs=P("section", "dp", "tensor"),
        check_vma=False,
    )
```

```python
import jax
import jax.numpy as jnp
from jax import lax
from jax.experimental import pallas as pl
from jax.experimental.pallas import tpu as pltpu
from jax.sharding import PartitionSpec as P

MESH = pl.DeviceIdType.MESH
N_DP, N_TENSOR, N_SECTION = 4, 16, 4
TOKENS = 24
PIECE = 2 * TOKENS
GROUP = 8 * PIECE
ROWS = N_TENSOR * PIECE
COLS = 2048
HALF = COLS // 2
WIDTH = 512
TILE = 2048
NEAR, FAR = 0, 1
RELAYED = (0, FAR)
ORDER = ((0, NEAR), (3, NEAR), (1, NEAR), (3, FAR), (2, NEAR), (1, FAR), (2, FAR), (0, FAR))
PARTS = 2


PLAN = (
    ("send", (0, NEAR)),
    ("send", (3, FAR)),
    ("send", (3, NEAR)),
    ("send", (1, FAR)),
    ("send", (1, NEAR)),
    ("send", (2, FAR)),
    ("send", (2, NEAR)),
    ("first", (0, NEAR)),
    ("first", (3, NEAR)),
    ("heads", None),
    ("second", (0, NEAR)),
    ("first", (1, NEAR)),
    ("second", (3, NEAR)),
    ("first", (3, FAR)),
    ("third", (0, NEAR)),
    ("second", (1, NEAR)),
    ("first", (2, NEAR)),
    ("third", (3, NEAR)),
    ("finish", (0, NEAR)),
    ("second", (3, FAR)),
    ("first", (1, FAR)),
    ("third", (1, NEAR)),
    ("relay", None),
    ("second", (2, NEAR)),
    ("first", (2, FAR)),
    ("third", (3, FAR)),
    ("heads2", None),
    ("finish", (3, NEAR)),
    ("second", (1, FAR)),
    ("first", (0, FAR)),
    ("third", (2, NEAR)),
    ("finish", (1, NEAR)),
    ("second", (2, FAR)),
    ("third", (1, FAR)),
    ("finish", (3, FAR)),
    ("second", (0, FAR)),
    ("third", (2, FAR)),
    ("heads3", None),
    ("finish", (1, FAR)),
    ("third", (0, FAR)),
    ("finish", (2, NEAR)),
    ("finish", (2, FAR)),
    ("finish", (0, FAR)),
)


def wrap(value, size):
    return lax.rem(value + size, size)


def kernel(
    order, grads, heads, out, a_all, b_all, acc, staged, heads_in, done,
    own_h, qs, qr, q1s, q1r, outs, s1s, s1r, rs, rr, x1s, x1r, x2s, x2r, dds, ddr, b1s, b1r, b2s, b2r,
):
    y = lax.axis_index("dp")
    t = lax.axis_index("tensor")
    s = lax.axis_index("section")
    x = lax.div(t, 4)
    h = lax.rem(lax.div(t, 2), 2)
    c = lax.rem(t, 2)
    z = 4 * h + s
    down, up = wrap(s - 1, 4), wrap(s + 1, 4)

    def tensor_of(xx, hh, cc):
        return xx * 4 + hh * 2 + cc

    def at_z(zz):
        return {"tensor": tensor_of(x, lax.div(zz, 4), c), "section": lax.rem(zz, 4)}

    to_z = (wrap(z - 1, 8), wrap(z + 3, 8))
    from_z = (wrap(z + 1, 8), wrap(z - 3, 8))
    from_h = tuple(lax.div(zz, 4) for zz in from_z)

    def rows_of(replica, xx, hh, cc):
        slot = replica * N_TENSOR + hh * 8 + xx * 2 + cc
        return pl.ds(pl.multiple_of(slot * PIECE, 16), PIECE)

    x_right, x_left, x_far = wrap(x + 1, 4), wrap(x - 1, 4), wrap(x + 2, 4)
    x_to = ({"tensor": tensor_of(x_right, h, c)}, {"tensor": tensor_of(x_left, h, c)})
    sibling = {"tensor": tensor_of(x, h, 1 - c)}
    y_up, y_down, y_far = wrap(y + 1, 4), wrap(y - 1, 4), wrap(y + 2, 4)
    y_to = ({"dp": y_up}, {"dp": y_down})

    own = pltpu.make_async_copy(heads, heads_in, own_h)
    own.start()

    barrier = pltpu.get_barrier_semaphore()

    def greet(device):
        pl.semaphore_signal(barrier, inc=1, device_id=device, device_id_type=MESH)

    for j in range(4):
        for n in (NEAR, FAR):
            if (j, n) != RELAYED:
                greet({"dp": wrap(y - j, 4), **at_z(from_z[n])})
    greet(at_z(wrap(z + 2, 8)))
    for device in (*x_to, sibling, *y_to):
        greet(device)
    pl.semaphore_wait(barrier, 13)

    def remote(src, dst, send, recv, device):
        return pltpu.make_async_remote_copy(
            src_ref=src, dst_ref=dst, send_sem=send, recv_sem=recv,
            device_id=device, device_id_type=MESH,
        )

    sends = []

    def go(copy):
        copy.start()
        sends.append(copy)

    def index(piece):
        return piece[0] * 2 + piece[1]

    def stage1(piece, part=None):
        j, n = piece
        target = wrap(y + j, 4)
        size = COLS if part is None else COLS // PARTS
        start = 0 if part is None else part * size
        return remote(
            grads.at[:, pl.ds(pl.multiple_of(target * COLS + start, size), size)],
            a_all.at[rows_of(y, x, h, c), pl.ds(start, size)],
            s1s.at[index(piece)] if part is None else qs.at[part],
            s1r.at[index(piece)] if part is None else qr.at[part],
            {"dp": target, **at_z(to_z[n])},
        )

    def stored(piece, xx, cc, half=None):
        j, n = piece
        rows = rows_of(wrap(y - j, 4), xx, from_h[n], cc)
        return a_all.at[rows, :] if half is None else a_all.at[rows, pl.ds(half * HALF, HALF)]

    def relay1():
        return remote(stored((RELAYED[0], NEAR), x, c), staged, rs.at[0], rr.at[0], at_z(wrap(z - 2, 8)))

    def relay2():
        rows = rows_of(wrap(y - RELAYED[0], 4), x, lax.div(wrap(z + 3, 8), 4), c)
        return remote(staged, a_all.at[rows, :], rs.at[1], rr.at[1], at_z(wrap(z - 2, 8)))

    def hop1(piece, way, xx, part=None):
        block = stored(piece, xx, c)
        if part is None:
            return remote(block, block, x1s.at[index(piece), way], x1r.at[index(piece), way], x_to[way])
        block = block.at[:, pl.ds(part * (COLS // PARTS), COLS // PARTS)]
        return remote(block, block, q1s.at[part, way], q1r.at[part, way], x_to[way])

    def hop2(piece, way, xx):
        block = stored(piece, xx, c, way)
        return remote(block, block, x2s.at[index(piece), way], x2r.at[index(piece), way], x_to[way])

    def across(piece, kind, cc):
        block = stored(piece, (x, x_left, x_right, x_far)[kind], cc)
        return remote(block, block, dds.at[index(piece), kind], ddr.at[index(piece), kind], sibling)

    def b_rows(replica, half=0, size=ROWS):
        return b_all.at[pl.ds(pl.multiple_of(replica * ROWS + half * (ROWS // 2), 128), size), :]

    def b_hop1(way, replica):
        block = b_rows(replica)
        return remote(block, block, b1s.at[way], b1r.at[way], y_to[way])

    def b_hop2(way, replica):
        block = b_rows(replica, way, ROWS // 2)
        return remote(block, block, b2s.at[way], b2r.at[way], y_to[way])

    def order_heads():
        own.wait()
        slots = (order[0, up], order[1, up])

        def place(slot, carry):
            source = tensor_of(lax.rem(lax.div(slot, 2), 4), lax.div(slot, 8), lax.rem(slot, 2))
            parts = [heads_in[m, source].astype(jnp.float32) for m in slots]
            rows = pl.ds(pl.multiple_of(y * ROWS + slot * PIECE, 16), PIECE)
            b_all[rows, :] = jnp.concatenate(parts, axis=0).astype(b_all.dtype)
            return carry

        lax.fori_loop(0, N_TENSOR, place, 0)

    def write(m):
        columns = pl.ds(pl.multiple_of(m * TILE, TILE), TILE)
        return pltpu.make_async_copy(done.at[columns, :], out.at[columns, :], outs.at[m])

    def compute(piece, first, last):
        j, n = piece
        start = wrap(y - j, 4) * ROWS + from_h[n] * GROUP
        rows = pl.ds(pl.multiple_of(start, GROUP), GROUP)

        def tile(m, carry):
            columns = pl.ds(pl.multiple_of(m * TILE, TILE), TILE)
            part = lax.dot_general(
                a_all[rows, columns], b_all[rows, :], (((0,), (0,)), ((), ())),
                preferred_element_type=jnp.float32,
            )
            if first:
                acc[columns, :] = part
            elif last:
                done[columns, :] = (acc[columns, :] + part).astype(done.dtype)
                write(m).start()
            else:
                acc[columns, :] += part
            return carry

        lax.fori_loop(0, COLS // TILE, tile, 0)

    def first(piece):
        if piece == ORDER[0]:
            for part in range(PARTS):
                stage1(piece, part).wait_recv()
                go(hop1(piece, 0, x, part))
                go(hop1(piece, 1, x, part))
            go(relay1())
        else:
            if piece == RELAYED:
                relay2().wait_recv()
            else:
                stage1(piece).wait_recv()
            go(hop1(piece, 0, x))
            go(hop1(piece, 1, x))
        go(across(piece, 0, c))

    def second(piece):
        for way, xx in ((0, x_left), (1, x_right)):
            if piece == ORDER[0]:
                for part in range(PARTS):
                    hop1(piece, way, xx, part).wait_recv()
            else:
                hop1(piece, way, xx).wait_recv()
            go(hop2(piece, way, xx))
            go(across(piece, 1 + way, c))

    def third(piece):
        hop2(piece, 0, x_far).wait_recv()
        hop2(piece, 1, x_far).wait_recv()
        go(across(piece, 3, c))

    def finish(piece):
        for kind in range(4):
            across(piece, kind, 1 - c).wait_recv()
        compute(piece, piece == ORDER[0], piece == ORDER[-1])

    paced = [piece for act, piece in PLAN if act == "sent"]
    for act, piece in PLAN:
        if act == "send":
            for copy in [stage1(piece, part) for part in range(PARTS)] if piece == ORDER[0] else [stage1(piece)]:
                copy.start()
                if piece not in paced:
                    sends.append(copy)
        elif act == "sent":
            stage1(piece).wait_send()
        elif act == "relay":
            relay1().wait_recv()
            go(relay2())
        elif act == "heads":
            order_heads()
            for way in (0, 1):
                go(b_hop1(way, y))
        elif act == "heads2":
            b_hop1(0, y_down).wait_recv()
            go(b_hop2(0, y_down))
            b_hop1(1, y_up).wait_recv()
            go(b_hop2(1, y_up))
        elif act == "heads3":
            for way in (0, 1):
                b_hop2(way, y_far).wait_recv()
        else:
            dict(first=first, second=second, third=third, finish=finish)[act](piece)
    for copy in sends:
        copy.wait_send()
    for m in range(COLS // TILE):
        write(m).wait()


def on_device(sent_grads, attn_out, b_order):
    grads = sent_grads[0, 0].reshape(PIECE, N_DP * COLS)
    heads = attn_out[0, 0].reshape(2, N_TENSOR, TOKENS, WIDTH)
    dma = pltpu.SemaphoreType.DMA
    result = pl.pallas_call(
        kernel,
        out_shape=jax.ShapeDtypeStruct((COLS, WIDTH), jnp.bfloat16),
        in_specs=[
            pl.BlockSpec(memory_space=pltpu.SMEM),
            pl.BlockSpec(memory_space=pltpu.HBM),
            pl.BlockSpec(memory_space=pltpu.HBM),
        ],
        out_specs=pl.BlockSpec(memory_space=pltpu.HBM),
        scratch_shapes=[
            pltpu.VMEM((N_DP * ROWS, COLS), jnp.bfloat16),
            pltpu.VMEM((N_DP * ROWS, WIDTH), jnp.bfloat16),
            pltpu.VMEM((COLS, WIDTH), jnp.float32),
            pltpu.VMEM((PIECE, COLS), jnp.bfloat16),
            pltpu.VMEM((2, N_TENSOR, TOKENS, WIDTH), jnp.bfloat16),
            pltpu.VMEM((COLS, WIDTH), jnp.bfloat16),
            dma, dma((PARTS,)), dma((PARTS,)), dma((PARTS, 2)), dma((PARTS, 2)), dma((COLS // TILE,)),
            dma((8,)), dma((8,)), dma((2,)), dma((2,)),
            dma((8, 2)), dma((8, 2)), dma((8, 2)), dma((8, 2)),
            dma((8, 4)), dma((8, 4)), dma((2,)), dma((2,)), dma((2,)), dma((2,)),
        ],
        compiler_params=pltpu.CompilerParams(
            collective_id=0, has_side_effects=True, vmem_limit_bytes=58 * 2**20
        ),
    )(b_order.T, grads, heads)
    return result[None]


def solution(mesh):
    placed = (
        P("section", "dp", None, "tensor", None),
        P("section", "dp", None, None, "tensor"),
        P(),
    )
    return jax.shard_map(
        on_device,
        mesh=mesh,
        in_specs=placed,
        out_specs=P("section", "dp", "tensor"),
        check_vma=False,
    )
```
